1024 devices in a mesh: gx: 4 (over y), gy: 8 (over z_hi, core), gz: 32 (over z_lo, x).
Axes of the slice: x: 4, y: 4, z: 32 (z_hi: 4, z_lo: 8; z = z_hi * 8 + z_lo), core: 2. Of those that a mesh axis runs over, the one named last changes fastest.
Arguments:
- offsets: float32 [4, 8, 32, 3, 128], P('gx', 'gy', 'gz'), may hold values from 0 to 10
- features: bfloat16 [4, 8, 32, 128, 256], P('gx', 'gy', 'gz'), may hold values from -6 to 6
- counts: int32 [4, 8, 32], P('gx', 'gy', 'gz'), may hold values from 64 to 128
- mask: int32 [4, 8, 32, 128], P('gx', 'gy', 'gz'), may hold values 0 or 1
- targets: float32 [4, 8, 32, 3, 128], P('gx', 'gy', 'gz'), may hold values from -6 to 6
- w_in: bfloat16 [256, 256], replicated, may hold values from -0.375 to 0.375
- radial: float32 [6, 256], replicated, may hold values from -5 to 5
- readout: float32 [256], replicated, may hold values from -0.375 to 0.375
Outputs:
- prediction: float32 [4, 8, 32, 3, 128], P('gx', 'gy', 'gz')
- grad_features: float32 [4, 8, 32, 128, 256], P('gx', 'gy', 'gz')
The draws below stay inside these ranges and needn't reach their ends.
All inputs are finite; a program needn't handle non-finite values. No bound on the sum of `mask` on one device may be relied on, other than what follows from the above.
Results may differ from the reference program's by a relative error of at most 0.0065.
Values may be sent and summed in bfloat16 or wider, within the bound.
A program may use at most 64 MiB of HBM per device.

```python
import jax
import jax.numpy as jnp
from jax import lax

F = 256
NB = 6
ATOM_DEV = 128
N_GX = 4
N_GY = 8
N_GZ = 32


def plant(entries, rng, least, top_value):
    longest = entries.shape.index(max(entries.shape))
    spots = []
    for shift in (0, 1):
        where = [jax.random.randint(jax.random.fold_in(rng, axis), (), 0, length) for axis, length in enumerate(entries.shape)]
        where[longest] = (where[longest] + shift) % entries.shape[longest]
        spots.append(tuple(where))
    return entries.at[spots[0]].set(least).at[spots[1]].set(top_value)


def level_of(key, shape, split, low, largest):
    def one(dim, parts):
        draws = jax.random.uniform(jax.random.fold_in(jax.random.fold_in(key, 6), dim), (parts,), jnp.float32, low / len(split), largest / len(split))
        return jnp.repeat(jnp.exp(draws), shape[dim] // parts).reshape((-1,) + (1,) * (len(shape) - dim - 1))

    gain = one(*split[0])
    for cut in split[1:]:
        gain = gain * one(*cut)
    return gain


def centred(stream_key, extent, deviation, bound, shards=(), kind=jnp.bfloat16):
    factor_of = level_of(stream_key, extent, shards, -0.22, 0.18) if shards else 1.0
    values = jax.random.normal(stream_key, extent, jnp.float32) * deviation * factor_of
    return jnp.minimum(jnp.maximum(values, -bound), bound).astype(kind)


def setup_inputs(seed: int = 0) -> dict:
    key_of = jax.random.split(jax.random.key(seed), 9)
    return {
        "offsets": jnp.clip(10.0 * jax.random.uniform(key_of[0], (N_GX, N_GY, N_GZ, 3, ATOM_DEV), jnp.float32) ** level_of(key_of[0], (N_GX, N_GY, N_GZ, 3, ATOM_DEV), ((0, 4), (1, 8), (2, 32)), -0.2, 0.2), 0.0, 10.0),
        "features": centred(key_of[1], (N_GX, N_GY, N_GZ, ATOM_DEV, F), 1.0, 6.0, ((0, 4), (1, 8), (2, 32))),
        "counts": plant(jax.random.randint(key_of[2], (N_GX, N_GY, N_GZ), ATOM_DEV // 2, ATOM_DEV + 1), jax.random.fold_in(key_of[2], 1), ATOM_DEV // 2, ATOM_DEV).astype(jnp.int32),
        "mask": plant((jax.random.randint(key_of[3], (N_GX, N_GY, N_GZ, ATOM_DEV), 0, 2) < 1).astype(jnp.int32), jax.random.fold_in(key_of[3], 1), 0, 1),
        "targets": centred(key_of[4], (N_GX, N_GY, N_GZ, 3, ATOM_DEV), 1.0, 6.0, ((0, 4), (1, 8), (2, 32)), jnp.float32),
        "w_in": centred(key_of[5], (F, F), F ** -0.5, 0.375),
        "radial": centred(key_of[6], (NB, F), 1.0, 5.0, (), jnp.float32),
        "readout": centred(key_of[7], (F,), F ** -0.5, 0.375, (), jnp.float32),
    }


EDGE = 10.0
CUT = 5.0
GAMMA = 20.0
LOSS_WEIGHT = 16.0


def slot_shift(first, count):
    slot = first + jnp.arange(count, dtype=jnp.int32)
    step_x = slot // 9 - 1
    step_y = (slot // 3) % 3 - 1
    step_z = slot % 3 - 1
    return jnp.stack([step_x, step_y, step_z], 1).astype(jnp.float32) * EDGE


def build_kernels(own, near, first, count, bases):
    atoms = own.shape[1]
    shift = slot_shift(first, count)
    placed = near[:, :3, :] + shift[:, :, None]
    placed = jnp.transpose(placed, (1, 0, 2)).reshape(3, count * atoms)
    weight_near = near[:, 3, :].reshape(count * atoms)
    apart = placed[:, None, :] - own[:3, :, None]
    ratio = (apart[0] * apart[0] + apart[1] * apart[1] + apart[2] * apart[2]) / (CUT * CUT)
    column = first * atoms + jnp.arange(count * atoms, dtype=jnp.int32)
    same = column[None, :] == (13 * atoms + jnp.arange(atoms, dtype=jnp.int32))[:, None]
    envelope = jnp.where(same, 0.0, jnp.square(jnp.maximum(1.0 - ratio, 0.0)))
    envelope = envelope * own[3][:, None] * weight_near[None, :]
    centers = jnp.arange(bases).astype(jnp.float32) / (bases - 1)
    radial_part = envelope[None] * jnp.exp(-GAMMA * jnp.square(ratio[None] - centers[:, None, None]))
    direction_part = envelope[None] * apart / CUT
    return jnp.concatenate([radial_part, direction_part], 0).astype(jnp.bfloat16)


def neighbours(grid, index):
    plane = N_GY * N_GZ
    pos_x = index // plane
    pos_y = (index // N_GZ) % N_GY
    pos_z = index % N_GZ
    slot = jnp.arange(27, dtype=jnp.int32)
    near_x = (pos_x + slot // 9 - 1) % N_GX
    near_y = (pos_y + (slot // 3) % 3 - 1) % N_GY
    near_z = (pos_z + slot % 3 - 1) % N_GZ
    return grid[near_x, near_y, near_z]


def reference(offsets, features, counts, mask, targets, w_in, radial, readout):
    bases = radial.shape[0]
    atoms = features.shape[3]
    width = features.shape[4]
    occ = (jnp.arange(atoms, dtype=jnp.int32)[None, None, None, :] < counts[..., None]).astype(jnp.float32)
    coords = jnp.concatenate([offsets, occ[:, :, :, None, :]], 3)
    proj = jnp.dot(features.reshape(-1, width), w_in, preferred_element_type=jnp.float32)
    proj = proj.astype(jnp.bfloat16).reshape(features.shape)
    flat_coords = coords.reshape(-1, 4, atoms)
    flat_mask = mask.reshape(-1, atoms).astype(jnp.float32)
    flat_targets = targets.reshape(-1, 3, atoms)
    hp = lax.Precision.HIGHEST
    count_all = N_GX * N_GY * N_GZ

    def forward_one(index):
        own = flat_coords[index]
        kern = build_kernels(own, neighbours(coords, index), 0, 27, bases)
        near_proj = neighbours(proj, index).reshape(27 * atoms, width)
        msg = jnp.einsum('kij,jf->kif', kern.astype(jnp.float32), near_proj.astype(jnp.float32))
        pre = jnp.einsum('bf,bif->if', radial, msg[:bases], precision=hp)
        gate = jax.nn.sigmoid(pre)
        gates = readout[None, :] * gate
        vec = msg[bases:]
        pred = jnp.einsum('cif,if->ci', vec, gates, precision=hp)
        err = LOSS_WEIGHT * flat_mask[index][None, :] * own[3][None, :] * (pred - flat_targets[index])
        slope = jnp.einsum('ci,cif->if', err, vec, precision=hp) * readout[None, :] * gate * (1.0 - gate)
        return pred, err, slope.astype(jnp.bfloat16), gates.astype(jnp.bfloat16)

    pred, err, slope, gates_bf = lax.map(forward_one, jnp.arange(count_all, dtype=jnp.int32))
    err_grid = err.reshape(N_GX, N_GY, N_GZ, 3, atoms)
    slope_grid = slope.reshape(N_GX, N_GY, N_GZ, atoms, width)
    gates_grid = gates_bf.reshape(N_GX, N_GY, N_GZ, atoms, width)

    def backward_one(index):
        own = flat_coords[index]
        kern = build_kernels(own, neighbours(coords, index), 0, 27, bases)
        near_err = jnp.transpose(neighbours(err_grid, index), (1, 0, 2)).reshape(3, 27 * atoms)
        near_slope = neighbours(slope_grid, index).reshape(27 * atoms, width)
        near_gates = neighbours(gates_grid, index).reshape(27 * atoms, width)
        wide = kern[bases:].astype(jnp.float32)
        pairs = wide[0] * near_err[0][None, :] + wide[1] * near_err[1][None, :] + wide[2] * near_err[2][None, :]
        pairs = pairs.astype(jnp.bfloat16)
        radial_sum = jnp.einsum('bij,jf->bif', kern[:bases].astype(jnp.float32), near_slope.astype(jnp.float32))
        cross = jnp.dot(pairs, near_gates, preferred_element_type=jnp.float32)
        back = jnp.einsum('bf,bif->if', radial, radial_sum, precision=hp) - cross
        return jnp.dot(back.astype(jnp.bfloat16), w_in.T, preferred_element_type=jnp.float32)

    grad = lax.map(backward_one, jnp.arange(count_all, dtype=jnp.int32))
    prediction = pred.reshape(N_GX, N_GY, N_GZ, 3, atoms)
    return prediction, grad.reshape(N_GX, N_GY, N_GZ, atoms, width)
```

```python
import math

import jax
import jax.numpy as jnp
from jax import lax
from jax.experimental import pallas as pl
from jax.experimental.pallas import tpu as pltpu
from jax.sharding import PartitionSpec as P

EDGE = 10.0
CUT = 5.0
GAMMA = 20.0
LOSS_WEIGHT = 16.0
FAR_AWAY = 1.0e4
MESH = pl.DeviceIdType.MESH
ROWS = 32

OWN, SIB, FAR = 0, 1, 2
STEPS = (0, -1, 1)
TARGETS = ((FAR, 1), (FAR, 2), (SIB, 1), (SIB, 2), (SIB, 0), (OWN, 1), (OWN, 2), (FAR, 0), (OWN, 0))


def slot(a, role, c):
    return role * 9 + a * 3 + c


def kernel(
    count_ref, offs_ref, feat_ref, mask_ref, targ_ref, w_ref, radial_ref, readout_ref,
    back_ref, pred_ref,
    proj, coords, rows_j, cols_i, kern_f, kern_b, msg, rhs, partial, acts, errs, zcols,
    part_sib, got_sib, part_gz, got_gz, part_far, got_far, send_sem, recv_sem,
):
    atoms, width = feat_ref.shape
    bases = radial_ref.shape[0]
    kinds = bases + 3
    f32, bf16 = jnp.float32, jnp.bfloat16
    gx, gy, gz = lax.axis_index("gx"), lax.axis_index("gy"), lax.axis_index("gz")
    nx, ny, nz = lax.axis_size("gx"), lax.axis_size("gy"), lax.axis_size("gz")
    core = gy % 2
    sib_gy = gy + 1 - 2 * core
    far_gy = (gy + ny - 1 + 2 * core) % ny
    sib = (gx, sib_gy, gz)
    far = (gx, far_gy, gz)
    to_gx = {1: ((gx + nx - 1) % nx, gy, gz), 2: ((gx + 1) % nx, gy, gz)}
    to_gz = {1: (gx, gy, (gz + nz - 1) % nz), 2: (gx, gy, (gz + 1) % nz)}
    flip = {1: 2, 2: 1}
    sib_step = (1 - 2 * core).astype(f32)
    role_step = (0.0, sib_step, -sib_step)

    barrier = pltpu.get_barrier_semaphore()
    for other in (far, to_gz[1], to_gz[2], to_gx[1], to_gx[2], sib):
        pl.semaphore_signal(barrier, inc=1, device_id=other, device_id_type=MESH)

    copies = {}

    def send(name, src, dst, device):
        index = len(copies)
        copy = pltpu.make_async_remote_copy(
            src_ref=src, dst_ref=dst, send_sem=send_sem.at[index], recv_sem=recv_sem.at[index],
            device_id=device, device_id_type=MESH,
        )
        copies[name] = copy
        copy.start()

    def wait(name):
        copies[name].wait_recv()

    def send_proj(a, role, c, to):
        here = proj.at[slot(a, role, c)]
        kind, d = to
        if kind == "sib":
            send(("p", a, SIB, c), here, proj.at[slot(a, SIB, c)], sib)
        elif kind == "far":
            send(("p", a, FAR, c), here, proj.at[slot(a, FAR, c)], far)
        elif kind == "gz":
            send(("p", a, role, flip[d]), here, proj.at[slot(a, role, flip[d])], to_gz[d])
        else:
            send(("p", flip[d], role, c), here, proj.at[slot(flip[d], role, c)], to_gx[d])

    lane = lax.broadcasted_iota(jnp.int32, (1, atoms), 1)
    occ_row = lane < count_ref[0]
    own = offs_ref[...] * (1.0 / CUT)
    coords[0, 0, OWN] = jnp.concatenate(
        [jnp.where(occ_row, own[0:1], FAR_AWAY), own[1:3], jnp.zeros((5, atoms), f32)], 0
    )
    proj[slot(0, OWN, 0)] = jnp.dot(
        feat_ref[...], w_ref[...], preferred_element_type=f32
    ).astype(bf16)

    pl.semaphore_wait(barrier, 6)

    send("c_far", coords.at[0, 0, OWN], coords.at[0, 0, FAR], far)
    send_proj(0, OWN, 0, ("far", 0))
    for d in (1, 2):
        send_proj(0, OWN, 0, ("gz", d))
    send("c_sib", coords.at[0, 0, OWN], coords.at[0, 0, SIB], sib)
    send_proj(0, OWN, 0, ("sib", 0))
    for d in (1, 2):
        send_proj(0, OWN, 0, ("gx", d))

    row_id = lax.broadcasted_iota(jnp.int32, (ROWS, atoms), 0)
    col_id = lax.broadcasted_iota(jnp.int32, (ROWS, atoms), 1)
    step = 2.0 * EDGE / (2.0 * CUT)

    def fill(block, xi, yi, zi, store, diag=None):
        dx = block[0:1] - xi
        dy = block[1:2] - yi
        dz = block[2:3] - zi
        ratio = dx * dx + dy * dy + dz * dz
        if diag is not None:
            ratio = ratio + diag
        room = jnp.maximum(1.0 - ratio, 0.0)
        near = 1.0 - room
        env = room * room
        grow = jnp.exp((2.0 * GAMMA / (bases - 1)) * near)
        value = env * jnp.exp(-GAMMA * (near * near))
        for k in range(bases):
            store(k, value.astype(bf16))
            if k < bases - 1:
                value = value * grow
        store(bases, (env * dx).astype(bf16))
        store(bases + 1, (env * dy).astype(bf16))
        store(bases + 2, (env * dz).astype(bf16))

    def place_rows(a, role, c):
        block = coords[a, c, role]
        r8 = lax.broadcasted_iota(jnp.int32, block.shape, 0)
        shift = jnp.where(
            r8 == 0, step * STEPS[a],
            jnp.where(r8 == 1, step * role_step[role], jnp.where(r8 == 2, step * STEPS[c], 0.0)),
        )
        rows_j[slot(a, role, c)] = block + shift

    def place_cols(blocks):
        stack = []
        for role, c in blocks:
            block = rows_j[slot(0, role, c)]
            r8 = lax.broadcasted_iota(jnp.int32, block.shape, 0)
            stack.append(jnp.where((r8 == 0) & (block > 0.5 * FAR_AWAY), -FAR_AWAY, block))
        if len(stack) < 16:
            stack.append(jnp.zeros((8 * (16 - len(stack)), atoms), f32))
        turned = jnp.transpose(jnp.concatenate(stack, 0))
        for n, where in enumerate(blocks):
            t = TARGETS.index(where)
            for axis in range(3):
                cols_i[t, axis] = jnp.broadcast_to(
                    turned[:, 8 * n + axis : 8 * n + axis + 1], (atoms, atoms)
                )

    own_t = TARGETS.index((OWN, 0))

    def forward_slots(slots, diag=False):
        for q in range(atoms // ROWS):
            at = slice(q * ROWS, (q + 1) * ROWS)
            xi, yi, zi = cols_i[own_t, 0, at], cols_i[own_t, 1, at], cols_i[own_t, 2, at]
            eye = jnp.where(row_id + q * ROWS == col_id, 4.0, 0.0) if diag else None
            for first, count, stride in slots:

                def one(n, unused, at=at, xi=xi, yi=yi, zi=zi, first=first, stride=stride, eye=eye):
                    s = first + n * stride
                    lanes = pl.ds(pl.multiple_of(s * atoms, atoms), atoms)

                    def store(k, value):
                        kern_f[k, at, lanes] = value

                    fill(rows_j[s], xi, yi, zi, store, eye)
                    return unused

                lax.fori_loop(0, count, one, 0)

    def backward_blocks(first, count, sources, diag=False):
        def one(n, unused):
            t = first + n // (atoms // ROWS)
            q = n % (atoms // ROWS)
            at = pl.ds(pl.multiple_of(q * ROWS, ROWS), ROWS)
            xi, yi, zi = cols_i[t, 0, at], cols_i[t, 1, at], cols_i[t, 2, at]
            eye = jnp.where(row_id + q * ROWS == col_id, 4.0, 0.0) if diag else None
            for a in sources:

                def store(k, value, a=a):
                    lo = (a * kinds + k) * atoms
                    kern_b[t, at, lo : lo + atoms] = value

                fill(rows_j[slot(a, OWN, 0)], xi, yi, zi, store, eye)
            return unused

        lax.fori_loop(0, count * (atoms // ROWS), one, 0)

    place_rows(0, OWN, 0)
    place_cols([(OWN, 0)])
    forward_slots([(slot(0, OWN, 0), 1, 1)], diag=True)

    wait("c_sib")
    wait(("p", 0, SIB, 0))
    for a in (1, 2):
        wait(("p", a, OWN, 0))
        send_proj(a, OWN, 0, ("sib", 0))
    wait("c_far")
    for d in (1, 2):
        send(("c_gz", flip[d]), coords.at[0, 0], coords.at[0, flip[d]], to_gz[d])
    place_rows(0, SIB, 0)
    place_rows(0, FAR, 0)
    forward_slots([(slot(0, SIB, 0), 2, 9)])
    for c in (1, 2):
        wait(("p", 0, OWN, c))
        for d in (1, 2):
            send_proj(0, OWN, c, ("gx", d))
        send_proj(0, OWN, c, ("sib", 0))
    wait(("p", 0, FAR, 0))
    for d in (1, 2):
        send_proj(0, FAR, 0, ("gz", d))
    for d in (1, 2):
        send_proj(0, FAR, 0, ("gx", d))
    for c in (1, 2):
        wait(("c_gz", c))
    for d in (1, 2):
        send(("c_gx", flip[d]), coords.at[0], coords.at[flip[d]], to_gx[d])
    for a in (1, 2):
        for c in (1, 2):
            wait(("p", a, OWN, c))
            send_proj(a, OWN, c, ("sib", 0))
    for role in (OWN, SIB, FAR):
        for c in (1, 2):
            place_rows(0, role, c)
    forward_slots([(slot(0, role, 1), 2, 1) for role in (OWN, SIB, FAR)])
    for c in (1, 2):
        wait(("p", 0, FAR, c))
        for d in (1, 2):
            send_proj(0, FAR, c, ("gx", d))
    for a in (1, 2):
        wait(("c_gx", a))
        for role in (OWN, SIB, FAR):
            for c in (0, 1, 2):
                place_rows(a, role, c)
    forward_slots([(slot(1, role, 0), 6, 1) for role in (OWN, SIB, FAR)])
    place_cols(list(TARGETS))
    backward_blocks(0, 8, (0, 1, 2))
    backward_blocks(8, 1, (0,), diag=True)
    backward_blocks(8, 1, (1, 2))

    for a in (0, 1, 2):
        for c in (0, 1, 2):
            if (a, c) != (0, 0):
                wait(("p", a, SIB, c))
    near = 18 * atoms
    msg[...] = jnp.dot(
        kern_f[:, :, :near].reshape(kinds * atoms, near),
        proj[0:18].reshape(near, width),
        preferred_element_type=f32,
    ).reshape(kinds, atoms, width)
    for a in (1, 2):
        for c in (0, 1, 2):
            wait(("p", a, FAR, c))
    msg[...] = msg[...] + jnp.dot(
        kern_f[:, :, near:].reshape(kinds * atoms, 9 * atoms),
        proj[18:27].reshape(9 * atoms, width),
        preferred_element_type=f32,
    ).reshape(kinds, atoms, width)

    weights = [
        radial_ref[b : b + 1] * math.exp(-GAMMA * (b / (bases - 1)) ** 2) for b in range(bases)
    ]
    readout = readout_ref[...]
    info = jnp.concatenate(
        [
            targ_ref[...],
            jnp.where(occ_row, mask_ref[...].astype(f32) * LOSS_WEIGHT, 0.0),
            jnp.zeros((atoms - 4, atoms), f32),
        ],
        0,
    )
    zcols[...] = jnp.transpose(info)
    for q in range(atoms // ROWS):
        at = slice(q * ROWS, (q + 1) * ROWS)
        pre = weights[0] * msg[0, at]
        for b in range(1, bases):
            pre = pre + weights[b] * msg[b, at]
        gate = jax.nn.sigmoid(pre)
        gates = readout * gate
        cols = zcols[at]
        scale = cols[:, 3:4]
        pull = jnp.zeros_like(pre)
        out = jnp.zeros((ROWS, atoms), f32)
        for c in range(3):
            vec = msg[bases + c, at]
            pred = jnp.sum(gates * vec, axis=1, keepdims=True)
            err = scale * (pred - cols[:, c : c + 1])
            pull = pull + err * vec
            out = jnp.where(col_id == c, pred, out)
            out = jnp.where(col_id == 3 + c, err, out)
        zcols[at] = out
        acts[0, 0, at] = (pull * readout * gate * (1.0 - gate)).astype(bf16)
        acts[0, 1, at] = gates.astype(bf16)
    turned = jnp.transpose(zcols[...])
    pred_ref[...] = turned[0:8]
    errs[0] = turned[0:8]

    for d in (1, 2):
        send(("act", flip[d]), acts.at[0], acts.at[flip[d]], to_gx[d])
        send(("err", flip[d]), errs.at[0], errs.at[flip[d]], to_gx[d])

    def build_rhs(a, cols, first):
        for q in range(atoms // ROWS):
            at = slice(q * ROWS, (q + 1) * ROWS)
            slope = acts[a, 0, at].astype(f32)
            gates = acts[a, 1, at].astype(f32)
            for b in range(bases):
                rhs[a * kinds + b, at] = (weights[b] * slope).astype(bf16)
            for c in range(3):
                err = cols[q * ROWS : (q + 1) * ROWS, first + c : first + c + 1]
                rhs[a * kinds + bases + c, at] = (gates * (-err)).astype(bf16)

    build_rhs(0, zcols[...], 3)
    part = kinds * atoms
    partial[...] = jnp.dot(
        kern_b[:, :, :part].reshape(9 * atoms, part),
        rhs[0:kinds].reshape(part, width),
        preferred_element_type=f32,
    ).reshape(9, atoms, width)
    for a in (1, 2):
        wait(("act", a))
        wait(("err", a))
    zcols[...] = jnp.transpose(
        jnp.concatenate([errs[1], errs[2], jnp.zeros((atoms - 16, atoms), f32)], 0)
    )
    build_rhs(1, zcols[...], 3)
    build_rhs(2, zcols[...], 11)

    def totals(first, count):
        return partial[first : first + count] + jnp.dot(
            kern_b[first : first + count, :, part:].reshape(count * atoms, 2 * part),
            rhs[kinds:].reshape(2 * part, width),
            preferred_element_type=f32,
        ).reshape(count, atoms, width)

    part_gz[1] = totals(0, 2).astype(bf16)
    for d in (1, 2):
        send(("far_gz", flip[d]), part_gz.at[1, d - 1], got_gz.at[1, flip[d] - 1], to_gz[d])
    part_sib[...] = totals(2, 3).astype(bf16)
    send("sib", part_sib, got_sib, sib)
    partial[5:7] = totals(5, 2)
    wait("sib")
    part_gz[0] = (partial[5:7] + got_sib[0:2].astype(f32)).astype(bf16)
    for d in (1, 2):
        send(("own_gz", flip[d]), part_gz.at[0, d - 1], got_gz.at[0, flip[d] - 1], to_gz[d])
    partial[7:9] = totals(7, 2)
    for c in (1, 2):
        wait(("far_gz", c))
    part_far[...] = (
        partial[7] + got_gz[1, 0].astype(f32) + got_gz[1, 1].astype(f32)
    ).astype(bf16)
    send("far", part_far, got_far, far)
    for c in (1, 2):
        wait(("own_gz", c))
    total = partial[8] + got_sib[2].astype(f32)
    total = total + got_gz[0, 0].astype(f32) + got_gz[0, 1].astype(f32)
    wait("far")
    back_ref[...] = (total + got_far[...].astype(f32)).astype(bf16)
    for copy in copies.values():
        copy.wait_send()


COPIES = 26 + 6 + 4 + 6


def on_device(offsets, features, counts, mask, targets, w_in, radial, readout):
    atoms, width = features.shape[3:]
    bases = radial.shape[0]
    kinds = bases + 3
    f32, bf16 = jnp.float32, jnp.bfloat16
    vmem = pl.BlockSpec(memory_space=pltpu.VMEM)
    back, pred = pl.pallas_call(
        kernel,
        out_shape=(
            jax.ShapeDtypeStruct((atoms, width), bf16),
            jax.ShapeDtypeStruct((8, atoms), f32),
        ),
        in_specs=[pl.BlockSpec(memory_space=pltpu.SMEM)] + [vmem] * 7,
        out_specs=(vmem, vmem),
        scratch_shapes=[
            pltpu.VMEM((27, atoms, width), bf16),
            pltpu.VMEM((3, 3, 3, 8, atoms), f32),
            pltpu.VMEM((27, 8, atoms), f32),
            pltpu.VMEM((9, 3, atoms, atoms), f32),
            pltpu.VMEM((kinds, atoms, 27 * atoms), bf16),
            pltpu.VMEM((9, atoms, 3 * kinds * atoms), bf16),
            pltpu.VMEM((kinds, atoms, width), f32),
            pltpu.VMEM((3 * kinds, atoms, width), bf16),
            pltpu.VMEM((9, atoms, width), f32),
            pltpu.VMEM((3, 2, atoms, width), bf16),
            pltpu.VMEM((3, 8, atoms), f32),
            pltpu.VMEM((atoms, atoms), f32),
            pltpu.VMEM((3, atoms, width), bf16),
            pltpu.VMEM((3, atoms, width), bf16),
            pltpu.VMEM((2, 2, atoms, width), bf16),
            pltpu.VMEM((2, 2, atoms, width), bf16),
            pltpu.VMEM((atoms, width), bf16),
            pltpu.VMEM((atoms, width), bf16),
            pltpu.SemaphoreType.DMA((COPIES,)),
            pltpu.SemaphoreType.DMA((COPIES,)),
        ],
        compiler_params=pltpu.CompilerParams(
            collective_id=0, has_side_effects=True, vmem_limit_bytes=48 << 20
        ),
        name="message_passing",
    )(
        counts.reshape(1),
        offsets.reshape(3, atoms),
        features.reshape(atoms, width),
        mask.reshape(1, atoms),
        targets.reshape(3, atoms),
        w_in,
        radial,
        readout.reshape(1, width),
    )
    grad = lax.dot_general(
        back, w_in, (((1,), (1,)), ((), ())), preferred_element_type=jnp.float32
    )
    return (pred[0:3].reshape(1, 1, 1, 3, atoms), grad.reshape(1, 1, 1, atoms, width))


def solution(mesh):
    in_specs = (
        P("gx", "gy", "gz", None, None),
        P("gx", "gy", "gz", None, None),
        P("gx", "gy", "gz"),
        P("gx", "gy", "gz", None),
        P("gx", "gy", "gz", None, None),
        P(),
        P(),
        P(),
    )
    out_specs = (P("gx", "gy", "gz", None, None), P("gx", "gy", "gz", None, None))
    return jax.shard_map(
        on_device, mesh=mesh, in_specs=in_specs, out_specs=out_specs, check_vma=False
    )
```

```python
import math

import jax
import jax.numpy as jnp
from jax import lax
from jax.experimental import pallas as pl
from jax.experimental.pallas import tpu as pltpu
from jax.sharding import PartitionSpec as P

EDGE = 10.0
CUT = 5.0
GAMMA = 20.0
LOSS_WEIGHT = 16.0
FAR_AWAY = 1.0e4
MESH = pl.DeviceIdType.MESH
ROWS = 32
RUN_X = 4

OWN, SIB, FAR = 0, 1, 2
STEPS = (0, -1, 1)
TARGETS = ((FAR, 1), (FAR, 2), (SIB, 1), (SIB, 2), (SIB, 0), (OWN, 1), (OWN, 2), (FAR, 0), (OWN, 0))


def slot(a, role, c):
    return role * 9 + a * 3 + c


def kernel(
    count_ref, offs_in, feat_in, mask_in, targ_in, w_in, radial_in, readout_in,
    back_ref, pred_ref,
    offs_ref, feat_ref, mask_ref, targ_ref, w_ref, radial_ref, readout_ref,
    proj, coords, rows_j, cols_i, kern_f, kern_b, msg, rhs, partial, acts, errs, zcols,
    part_sib, got_sib, part_gz, got_gz, part_far, got_far, send_sem, recv_sem, load_sem,
):
    atoms, width = feat_ref.shape
    bases = radial_ref.shape[0]
    kinds = bases + 3
    f32, bf16 = jnp.float32, jnp.bfloat16
    gx, gy, gz = lax.axis_index("gx"), lax.axis_index("gy"), lax.axis_index("gz")
    nx, ny, nz = lax.axis_size("gx"), lax.axis_size("gy"), lax.axis_size("gz")
    core = gy % 2
    sib_gy = gy + 1 - 2 * core
    far_gy = (gy + ny - 1 + 2 * core) % ny
    sib = (gx, sib_gy, gz)
    far = (gx, far_gy, gz)
    to_gx = {1: ((gx + nx - 1) % nx, gy, gz), 2: ((gx + 1) % nx, gy, gz)}
    to_gz = {1: (gx, gy, (gz + nz - 1) % nz), 2: (gx, gy, (gz + 1) % nz)}
    flip = {1: 2, 2: 1}
    cross = {1: gz % RUN_X == 0, 2: gz % RUN_X == RUN_X - 1}
    inside = {1: gz % RUN_X != 0, 2: gz % RUN_X != RUN_X - 1}
    seam = {1: gz == 0, 2: gz == nz - 1}
    no_seam = {1: gz != 0, 2: gz != nz - 1}
    edge = {1: (gz % RUN_X == 0) & (gz != 0), 2: (gz % RUN_X == RUN_X - 1) & (gz != nz - 1)}
    on_seam = {1: 1 - (gz + nz - 1) // nz, 2: (gz + 1) // nz}
    sib_step = (1 - 2 * core).astype(f32)
    role_step = (0.0, sib_step, -sib_step)

    barrier = pltpu.get_barrier_semaphore()
    for other in (far, to_gz[1], to_gz[2], to_gx[1], to_gx[2], sib):
        pl.semaphore_signal(barrier, inc=1, device_id=other, device_id_type=MESH)

    loads = [
        pltpu.make_async_copy(src, dst, load_sem.at[n])
        for n, (src, dst) in enumerate(
            (
                (feat_in, feat_ref), (w_in, w_ref), (offs_in, offs_ref), (mask_in, mask_ref),
                (targ_in, targ_ref), (radial_in, radial_ref), (readout_in, readout_ref),
            )
        )
    ]
    for load in loads:
        load.start()

    copies = {}

    def copy_of(name, src, dst, device):
        index = len(copies)
        copies[name] = pltpu.make_async_remote_copy(
            src_ref=src, dst_ref=dst, send_sem=send_sem.at[index], recv_sem=recv_sem.at[index],
            device_id=device, device_id_type=MESH,
        )

    def wait(name):
        copies[name].wait_recv()

    def start(name):
        copies[name].start()

    def sends(name, src, dst, device):
        copy_of(name, src, dst, device)
        start(name)

    here = lambda a, role, c: proj.at[slot(a, role, c)]
    copy_of(("p", 0, FAR, 0), here(0, OWN, 0), here(0, FAR, 0), far)
    for d in (1, 2):
        for role in (OWN, FAR):
            copy_of(("p", 0, role, flip[d]), here(0, role, 0), here(0, role, flip[d]), to_gz[d])
            for c in (0, 1, 2):
                copy_of(("p", flip[d], role, c), here(0, role, c), here(flip[d], role, c), to_gx[d])
    for a in (0, 1, 2):
        for c in (0, 1, 2):
            copy_of(("p", a, SIB, c), here(a, OWN, c), here(a, SIB, c), sib)

    for load in loads:
        load.wait()
    lane = lax.broadcasted_iota(jnp.int32, (1, atoms), 1)
    occ_row = lane < count_ref[0]
    own = [offs_ref[axis] * (1.0 / CUT) for axis in range(3)]
    coords[0, 0, OWN] = jnp.concatenate(
        [jnp.where(occ_row, own[0], FAR_AWAY), own[1], own[2], jnp.zeros((5, atoms), f32)], 0
    )
    proj[slot(0, OWN, 0)] = jnp.dot(
        feat_ref[...], w_ref[...], preferred_element_type=f32
    ).astype(bf16)

    pl.semaphore_wait(barrier, 6)

    sends("c_far", coords.at[0, 0, OWN], coords.at[0, 0, FAR], far)
    start(("p", 0, FAR, 0))
    sends("c_sib", coords.at[0, 0, OWN], coords.at[0, 0, SIB], sib)
    for d in (1, 2):
        pl.when(inside[d])(lambda d=d: start(("p", 0, OWN, flip[d])))
    for d in (1, 2):
        start(("p", flip[d], OWN, 0))
    start(("p", 0, SIB, 0))

    row_id = lax.broadcasted_iota(jnp.int32, (ROWS, atoms), 0)
    col_id = lax.broadcasted_iota(jnp.int32, (ROWS, atoms), 1)
    step = 2.0 * EDGE / (2.0 * CUT)

    def fill(block, xi, yi, zi, store, diag=None):
        dx = block[0:1] - xi
        dy = block[1:2] - yi
        dz = block[2:3] - zi
        ratio = dx * dx + dy * dy + dz * dz
        if diag is not None:
            ratio = ratio + diag
        room = jnp.maximum(1.0 - ratio, 0.0)
        near = 1.0 - room
        env = room * room
        grow = jnp.exp((2.0 * GAMMA / (bases - 1)) * near)
        value = env * jnp.exp(-GAMMA * (near * near))
        for k in range(bases):
            store(k, value.astype(bf16))
            if k < bases - 1:
                value = value * grow
        store(bases, (env * dx).astype(bf16))
        store(bases + 1, (env * dy).astype(bf16))
        store(bases + 2, (env * dz).astype(bf16))

    def place_rows(a, role, c):
        block = coords[a, c, role]
        r8 = lax.broadcasted_iota(jnp.int32, block.shape, 0)
        shift = jnp.where(
            r8 == 0, step * STEPS[a],
            jnp.where(r8 == 1, step * role_step[role], jnp.where(r8 == 2, step * STEPS[c], 0.0)),
        )
        rows_j[slot(a, role, c)] = block + shift

    def place_cols(blocks):
        stack = []
        for role, c in blocks:
            block = rows_j[slot(0, role, c)]
            r8 = lax.broadcasted_iota(jnp.int32, block.shape, 0)
            stack.append(jnp.where((r8 == 0) & (block > 0.5 * FAR_AWAY), -FAR_AWAY, block))
        if len(stack) < 16:
            stack.append(jnp.zeros((8 * (16 - len(stack)), atoms), f32))
        turned = jnp.transpose(jnp.concatenate(stack, 0))
        for n, where in enumerate(blocks):
            t = TARGETS.index(where)
            for axis in range(3):
                cols_i[t, axis] = jnp.broadcast_to(
                    turned[:, 8 * n + axis : 8 * n + axis + 1], (atoms, atoms)
                )

    own_t = TARGETS.index((OWN, 0))

    def forward_slots(slots, diag=False):
        for q in range(atoms // ROWS):
            at = slice(q * ROWS, (q + 1) * ROWS)
            xi, yi, zi = cols_i[own_t, 0, at], cols_i[own_t, 1, at], cols_i[own_t, 2, at]
            eye = jnp.where(row_id + q * ROWS == col_id, 4.0, 0.0) if diag else None
            for first, count, stride in slots:

                def one(n, unused, at=at, xi=xi, yi=yi, zi=zi, first=first, stride=stride, eye=eye):
                    s = first + n * stride
                    lanes = pl.ds(pl.multiple_of(s * atoms, atoms), atoms)

                    def store(k, value):
                        kern_f[k, at, lanes] = value

                    fill(rows_j[s], xi, yi, zi, store, eye)
                    return unused

                lax.fori_loop(0, count, one, 0)

    def backward_blocks(first, count, sources, diag=False):
        def one(n, unused):
            t = first + n // (atoms // ROWS)
            q = n % (atoms // ROWS)
            at = pl.ds(pl.multiple_of(q * ROWS, ROWS), ROWS)
            xi, yi, zi = cols_i[t, 0, at], cols_i[t, 1, at], cols_i[t, 2, at]
            eye = jnp.where(row_id + q * ROWS == col_id, 4.0, 0.0) if diag else None
            for a in sources:

                def store(k, value, a=a):
                    lo = (a * kinds + k) * atoms
                    kern_b[t, at, lo : lo + atoms] = value

                fill(rows_j[slot(a, OWN, 0)], xi, yi, zi, store, eye)
            return unused

        lax.fori_loop(0, count * (atoms // ROWS), one, 0)

    def pass_own(c):
        wait(("p", 0, OWN, c))
        for d in (1, 2):
            start(("p", flip[d], OWN, c))
        start(("p", 0, SIB, c))

    def pass_sib(c):
        for a in (1, 2):
            wait(("p", a, OWN, c))
            start(("p", a, SIB, c))

    def pass_far(c):
        wait(("p", 0, FAR, c))
        for d in (1, 2):
            start(("p", flip[d], FAR, c))

    place_rows(0, OWN, 0)
    place_cols([(OWN, 0)])
    forward_slots([(slot(0, OWN, 0), 1, 1)], diag=True)
    backward_blocks(8, 1, (0,), diag=True)

    wait("c_sib")
    for d in (1, 2):
        sends(("c_gz1", flip[d]), coords.at[0, 0, 0:2], coords.at[0, flip[d], 0:2], to_gz[d])
    pass_sib(0)
    for c in (1, 2):
        pl.when(inside[c])(lambda c=c: pass_own(c))
    place_rows(0, SIB, 0)
    forward_slots([(slot(0, SIB, 0), 1, 1)])

    wait("c_far")
    for d in (1, 2):
        sends(("c_gz2", flip[d]), coords.at[0, 0, FAR], coords.at[0, flip[d], FAR], to_gz[d])
    for d in (1, 2):
        pl.when(cross[d])(lambda d=d: start(("p", 0, OWN, flip[d])))
    for c in (1, 2):
        wait(("c_gz1", c))
    for d in (1, 2):
        sends(("c_gx1", flip[d]), coords.at[0, :, 0:2], coords.at[flip[d], :, 0:2], to_gx[d])
    for c in (1, 2):
        pl.when(inside[c])(lambda c=c: pass_sib(c))
    for role in (OWN, SIB):
        for c in (1, 2):
            place_rows(0, role, c)
    place_rows(0, FAR, 0)
    forward_slots([(slot(0, role, 1), 2, 1) for role in (OWN, SIB)])
    for a in (1, 2):
        wait(("c_gx1", a))
        for role in (OWN, SIB):
            for c in (0, 1, 2):
                place_rows(a, role, c)
    forward_slots([(slot(1, role, 0), 6, 1) for role in (OWN, SIB)])

    wait(("p", 0, FAR, 0))
    for d in (1, 2):
        start(("p", 0, FAR, flip[d]))
    for d in (1, 2):
        start(("p", flip[d], FAR, 0))
    for c in (1, 2):
        wait(("c_gz2", c))
        place_rows(0, FAR, c)
    for d in (1, 2):
        sends(("c_gx2", flip[d]), coords.at[0, :, FAR], coords.at[flip[d], :, FAR], to_gx[d])
    forward_slots([(slot(0, FAR, 0), 1, 1)])
    place_cols([where for where in TARGETS if where != (OWN, 0)])
    backward_blocks(2, 5, (0, 1, 2))
    for c in (1, 2):
        pl.when(inside[c])(lambda c=c: pass_far(c))

    def cross_pass(c):
        pass_own(c)
        pass_far(c)

    for c in (1, 2):
        pl.when(edge[c])(lambda c=c: cross_pass(c))
    for c in (1, 2):
        pl.when(edge[c])(lambda c=c: pass_sib(c))
    for a in (1, 2):
        wait(("c_gx2", a))
        for c in (0, 1, 2):
            place_rows(a, FAR, c)
    forward_slots([(slot(0, FAR, 1), 8, 1)])
    backward_blocks(0, 2, (0, 1, 2))
    backward_blocks(7, 1, (0, 1, 2))
    backward_blocks(8, 1, (1, 2))
    for c in (1, 2):
        pl.when(seam[c])(lambda c=c: pass_own(c))
    for c in (1, 2):
        pl.when(seam[c])(lambda c=c: pass_sib(c))
    for c in (1, 2):
        pl.when(seam[c])(lambda c=c: pass_far(c))

    for a in (0, 1, 2):
        for c in (0, 1, 2):
            wait(("p", a, SIB, c))
    near = 18 * atoms
    msg[...] = jnp.dot(
        kern_f[:, :, :near].reshape(kinds * atoms, near),
        proj[0:18].reshape(near, width),
        preferred_element_type=f32,
    ).reshape(kinds, atoms, width)
    for a in (1, 2):
        for c in (0, 1, 2):
            wait(("p", a, FAR, c))
    msg[...] = msg[...] + jnp.dot(
        kern_f[:, :, near:].reshape(kinds * atoms, 9 * atoms),
        proj[18:27].reshape(9 * atoms, width),
        preferred_element_type=f32,
    ).reshape(kinds, atoms, width)

    weights = [
        radial_ref[b : b + 1] * math.exp(-GAMMA * (b / (bases - 1)) ** 2) for b in range(bases)
    ]
    readout = readout_ref[...]
    info = jnp.concatenate(
        [
            targ_ref[0], targ_ref[1], targ_ref[2],
            jnp.where(occ_row, mask_ref[...].astype(f32) * LOSS_WEIGHT, 0.0),
            jnp.zeros((atoms - 4, atoms), f32),
        ],
        0,
    )
    zcols[...] = jnp.transpose(info)
    for q in range(atoms // ROWS):
        at = slice(q * ROWS, (q + 1) * ROWS)
        pre = weights[0] * msg[0, at]
        for b in range(1, bases):
            pre = pre + weights[b] * msg[b, at]
        gate = jax.nn.sigmoid(pre)
        gates = readout * gate
        cols = zcols[at]
        scale = cols[:, 3:4]
        pull = jnp.zeros_like(pre)
        out = jnp.zeros((ROWS, atoms), f32)
        for c in range(3):
            vec = msg[bases + c, at]
            pred = jnp.sum(gates * vec, axis=1, keepdims=True)
            err = scale * (pred - cols[:, c : c + 1])
            pull = pull + err * vec
            out = jnp.where(col_id == c, pred, out)
            out = jnp.where(col_id == 3 + c, err, out)
        zcols[at] = out
        acts[0, 0, at] = (pull * readout * gate * (1.0 - gate)).astype(bf16)
        acts[0, 1, at] = gates.astype(bf16)
    turned = jnp.transpose(zcols[...])
    for c in range(3):
        pred_ref[c] = turned[c : c + 1]
    errs[0] = turned[0:8]

    for d in (1, 2):
        sends(("act", flip[d]), acts.at[0], acts.at[flip[d]], to_gx[d])
        sends(("err", flip[d]), errs.at[0], errs.at[flip[d]], to_gx[d])

    def build_rhs(a, cols, first):
        for q in range(atoms // ROWS):
            at = slice(q * ROWS, (q + 1) * ROWS)
            slope = acts[a, 0, at].astype(f32)
            gates = acts[a, 1, at].astype(f32)
            for b in range(bases):
                rhs[a * kinds + b, at] = (weights[b] * slope).astype(bf16)
            for c in range(3):
                err = cols[q * ROWS : (q + 1) * ROWS, first + c : first + c + 1]
                rhs[a * kinds + bases + c, at] = (gates * (-err)).astype(bf16)

    build_rhs(0, zcols[...], 3)
    part = kinds * atoms
    partial[...] = jnp.dot(
        kern_b[:, :, :part].reshape(9 * atoms, part),
        rhs[0:kinds].reshape(part, width),
        preferred_element_type=f32,
    ).reshape(9, atoms, width)
    for a in (1, 2):
        wait(("act", a))
        wait(("err", a))
    zcols[...] = jnp.transpose(
        jnp.concatenate([errs[1], errs[2], jnp.zeros((atoms - 16, atoms), f32)], 0)
    )
    build_rhs(1, zcols[...], 3)
    build_rhs(2, zcols[...], 11)

    def totals(first, count):
        return partial[first : first + count] + jnp.dot(
            kern_b[first : first + count, :, part:].reshape(count * atoms, 2 * part),
            rhs[kinds:].reshape(2 * part, width),
            preferred_element_type=f32,
        ).reshape(count, atoms, width)

    part_gz[1] = totals(0, 2).astype(bf16)
    for d in (1, 2):
        gx_d, gy_d, gz_d = to_gz[d]
        device = (gx_d, gy_d + on_seam[d] * (far_gy - gy_d), gz_d)
        sends(("far_gz", flip[d]), part_gz.at[1, d - 1], got_gz.at[1, flip[d] - 1], device)
    partial[7] = totals(7, 1)[0]
    part_sib[...] = totals(2, 3).astype(bf16)
    sends("sib", part_sib, got_sib, sib)

    def add_far_gz(c, n):
        wait(("far_gz", c))
        partial[n] = partial[n] + got_gz[1, c - 1].astype(f32)

    for c in (1, 2):
        pl.when(no_seam[c])(lambda c=c: add_far_gz(c, 7))
    part_far[...] = partial[7].astype(bf16)
    sends("far", part_far, got_far, far)
    partial[5:7] = totals(5, 2)
    wait("sib")
    part_gz[0] = (partial[5:7] + got_sib[0:2].astype(f32)).astype(bf16)
    for d in (1, 2):
        sends(("own_gz", flip[d]), part_gz.at[0, d - 1], got_gz.at[0, flip[d] - 1], to_gz[d])
    partial[8] = totals(8, 1)[0] + got_sib[2].astype(f32)
    for c in (1, 2):
        wait(("own_gz", c))
    partial[8] = partial[8] + got_gz[0, 0].astype(f32) + got_gz[0, 1].astype(f32)
    for c in (1, 2):
        pl.when(seam[c])(lambda c=c: add_far_gz(c, 8))
    wait("far")
    back_ref[...] = (partial[8] + got_far[...].astype(f32)).astype(bf16)
    for copy in copies.values():
        copy.wait_send()


COPIES = 26 + 10 + 4 + 6


def on_device(offsets, features, counts, mask, targets, w_in, radial, readout):
    atoms, width = features.shape[3:]
    bases = radial.shape[0]
    kinds = bases + 3
    f32, bf16 = jnp.float32, jnp.bfloat16
    vmem = pl.BlockSpec(memory_space=pltpu.VMEM)
    back, pred = pl.pallas_call(
        kernel,
        out_shape=(
            jax.ShapeDtypeStruct((atoms, width), bf16),
            jax.ShapeDtypeStruct((3, 1, atoms), f32),
        ),
        in_specs=[pl.BlockSpec(memory_space=pltpu.SMEM)] + [pl.BlockSpec(memory_space=pl.ANY)] * 7,
        out_specs=(vmem, vmem),
        scratch_shapes=[
            pltpu.VMEM((3, 1, atoms), f32),
            pltpu.VMEM((atoms, width), bf16),
            pltpu.VMEM((1, atoms), jnp.int32),
            pltpu.VMEM((3, 1, atoms), f32),
            pltpu.VMEM(w_in.shape, bf16),
            pltpu.VMEM(radial.shape, f32),
            pltpu.VMEM((1, width), f32),
            pltpu.VMEM((27, atoms, width), bf16),
            pltpu.VMEM((3, 3, 3, 8, atoms), f32),
            pltpu.VMEM((27, 8, atoms), f32),
            pltpu.VMEM((9, 3, atoms, atoms), f32),
            pltpu.VMEM((kinds, atoms, 27 * atoms), bf16),
            pltpu.VMEM((9, atoms, 3 * kinds * atoms), bf16),
            pltpu.VMEM((kinds, atoms, width), f32),
            pltpu.VMEM((3 * kinds, atoms, width), bf16),
            pltpu.VMEM((9, atoms, width), f32),
            pltpu.VMEM((3, 2, atoms, width), bf16),
            pltpu.VMEM((3, 8, atoms), f32),
            pltpu.VMEM((atoms, atoms), f32),
            pltpu.VMEM((3, atoms, width), bf16),
            pltpu.VMEM((3, atoms, width), bf16),
            pltpu.VMEM((2, 2, atoms, width), bf16),
            pltpu.VMEM((2, 2, atoms, width), bf16),
            pltpu.VMEM((atoms, width), bf16),
            pltpu.VMEM((atoms, width), bf16),
            pltpu.SemaphoreType.DMA((COPIES,)),
            pltpu.SemaphoreType.DMA((COPIES,)),
            pltpu.SemaphoreType.DMA((7,)),
        ],
        compiler_params=pltpu.CompilerParams(
            collective_id=0, has_side_effects=True, vmem_limit_bytes=60 << 20
        ),
        name="message_passing",
    )(
        counts.reshape(1),
        offsets.reshape(3, 1, atoms),
        features.reshape(atoms, width),
        mask.reshape(1, atoms),
        targets.reshape(3, 1, atoms),
        w_in,
        radial,
        readout.reshape(1, width),
    )
    grad = lax.dot_general(
        back, w_in, (((1,), (1,)), ((), ())), preferred_element_type=jnp.float32
    )
    return (pred.reshape(1, 1, 1, 3, atoms), grad.reshape(1, 1, 1, atoms, width))


def solution(mesh):
    in_specs = (
        P("gx", "gy", "gz", None, None),
        P("gx", "gy", "gz", None, None),
        P("gx", "gy", "gz"),
        P("gx", "gy", "gz", None),
        P("gx", "gy", "gz", None, None),
        P(),
        P(),
        P(),
    )
    out_specs = (P("gx", "gy", "gz", None, None), P("gx", "gy", "gz", None, None))
    return jax.shard_map(
        on_device, mesh=mesh, in_specs=in_specs, out_specs=out_specs, check_vma=False
    )
```

```python
import math

import jax
import jax.numpy as jnp
from jax import lax
from jax.experimental import pallas as pl
from jax.experimental.pallas import tpu as pltpu
from jax.sharding import PartitionSpec as P

EDGE = 10.0
CUT = 5.0
GAMMA = 20.0
LOSS_WEIGHT = 16.0
FAR_AWAY = 1.0e4
MESH = pl.DeviceIdType.MESH
ROWS = 32
RUN_X = 4

OWN, SIB, FAR = 0, 1, 2
STEPS = (0, -1, 1)
TARGETS = ((FAR, 1), (FAR, 2), (SIB, 1), (SIB, 2), (SIB, 0), (OWN, 1), (OWN, 2), (FAR, 0), (OWN, 0))


def slot(a, role, c):
    return 18 + c * 3 + a if role == FAR else c * 6 + a * 2 + role


def kernel(
    count_ref, offs_in, feat_in, mask_in, targ_in, w_in, radial_in, readout_in,
    back_ref, pred_ref,
    offs_ref, feat_ref, mask_ref, targ_ref, w_ref, radial_ref, readout_ref,
    proj, coords, rows_j, cols_i, kern_f, kern_b, msg, rhs, partial, acts, errs, zcols,
    part_sib, got_sib, part_gz, got_gz, part_far, got_far, send_sem, recv_sem, load_sem,
):
    atoms, width = feat_ref.shape
    bases = radial_ref.shape[0]
    kinds = bases + 3
    f32, bf16 = jnp.float32, jnp.bfloat16
    gx, gy, gz = lax.axis_index("gx"), lax.axis_index("gy"), lax.axis_index("gz")
    nx, ny, nz = lax.axis_size("gx"), lax.axis_size("gy"), lax.axis_size("gz")
    core = gy % 2
    sib_gy = gy + 1 - 2 * core
    far_gy = (gy + ny - 1 + 2 * core) % ny
    sib = (gx, sib_gy, gz)
    far = (gx, far_gy, gz)
    to_gx = {1: ((gx + nx - 1) % nx, gy, gz), 2: ((gx + 1) % nx, gy, gz)}
    to_gz = {1: (gx, gy, (gz + nz - 1) % nz), 2: (gx, gy, (gz + 1) % nz)}
    flip = {1: 2, 2: 1}
    cross = {1: gz % RUN_X == 0, 2: gz % RUN_X == RUN_X - 1}
    inside = {1: gz % RUN_X != 0, 2: gz % RUN_X != RUN_X - 1}
    seam = {1: gz == 0, 2: gz == nz - 1}
    no_seam = {1: gz != 0, 2: gz != nz - 1}
    edge = {1: (gz % RUN_X == 0) & (gz != 0), 2: (gz % RUN_X == RUN_X - 1) & (gz != nz - 1)}
    on_seam = {1: 1 - (gz + nz - 1) // nz, 2: (gz + 1) // nz}
    sib_step = (1 - 2 * core).astype(f32)
    role_step = (0.0, sib_step, -sib_step)

    barrier = pltpu.get_barrier_semaphore()
    for other in (far, to_gz[1], to_gz[2], to_gx[1], to_gx[2], sib):
        pl.semaphore_signal(barrier, inc=1, device_id=other, device_id_type=MESH)

    loads = [
        pltpu.make_async_copy(src, dst, load_sem.at[n])
        for n, (src, dst) in enumerate(
            (
                (feat_in, feat_ref), (w_in, w_ref), (offs_in, offs_ref), (mask_in, mask_ref),
                (targ_in, targ_ref), (radial_in, radial_ref), (readout_in, readout_ref),
            )
        )
    ]
    for load in loads:
        load.start()

    copies = {}

    def copy_of(name, src, dst, device):
        index = len(copies)
        copies[name] = pltpu.make_async_remote_copy(
            src_ref=src, dst_ref=dst, send_sem=send_sem.at[index], recv_sem=recv_sem.at[index],
            device_id=device, device_id_type=MESH,
        )

    def wait(name):
        copies[name].wait_recv()

    def start(name):
        copies[name].start()

    def sends(name, src, dst, device):
        copy_of(name, src, dst, device)
        start(name)

    here = lambda a, role, c: proj.at[slot(a, role, c)]
    copy_of(("p", 0, FAR, 0), here(0, OWN, 0), here(0, FAR, 0), far)
    for d in (1, 2):
        for role in (OWN, FAR):
            copy_of(("p", 0, role, flip[d]), here(0, role, 0), here(0, role, flip[d]), to_gz[d])
            for c in (0, 1, 2):
                copy_of(("p", flip[d], role, c), here(0, role, c), here(flip[d], role, c), to_gx[d])
    for a in (0, 1, 2):
        for c in (0, 1, 2):
            copy_of(("p", a, SIB, c), here(a, OWN, c), here(a, SIB, c), sib)

    for load in loads:
        load.wait()
    lane = lax.broadcasted_iota(jnp.int32, (1, atoms), 1)
    occ_row = lane < count_ref[0]
    own = [offs_ref[axis] * (1.0 / CUT) for axis in range(3)]
    coords[0, 0, OWN] = jnp.concatenate(
        [jnp.where(occ_row, own[0], FAR_AWAY), own[1], own[2], jnp.zeros((5, atoms), f32)], 0
    )
    proj[slot(0, OWN, 0)] = jnp.dot(
        feat_ref[...], w_ref[...], preferred_element_type=f32
    ).astype(bf16)

    pl.semaphore_wait(barrier, 6)

    sends("c_far", coords.at[0, 0, OWN], coords.at[0, 0, FAR], far)
    start(("p", 0, FAR, 0))
    sends("c_sib", coords.at[0, 0, OWN], coords.at[0, 0, SIB], sib)
    for d in (1, 2):
        pl.when(inside[d])(lambda d=d: start(("p", 0, OWN, flip[d])))
    for d in (1, 2):
        start(("p", flip[d], OWN, 0))
    start(("p", 0, SIB, 0))

    row_id = lax.broadcasted_iota(jnp.int32, (ROWS, atoms), 0)
    col_id = lax.broadcasted_iota(jnp.int32, (ROWS, atoms), 1)
    step = 2.0 * EDGE / (2.0 * CUT)

    def fill(block, xi, yi, zi, store, diag=None):
        dx = block[0:1] - xi
        dy = block[1:2] - yi
        dz = block[2:3] - zi
        ratio = dx * dx + dy * dy + dz * dz
        if diag is not None:
            ratio = ratio + diag
        room = jnp.maximum(1.0 - ratio, 0.0)
        near = 1.0 - room
        env = room * room
        grow = jnp.exp((2.0 * GAMMA / (bases - 1)) * near)
        value = env * jnp.exp(-GAMMA * (near * near))
        for k in range(bases):
            store(k, value.astype(bf16))
            if k < bases - 1:
                value = value * grow
        store(bases, (env * dx).astype(bf16))
        store(bases + 1, (env * dy).astype(bf16))
        store(bases + 2, (env * dz).astype(bf16))

    def place_rows(a, role, c):
        block = coords[a, c, role]
        r8 = lax.broadcasted_iota(jnp.int32, block.shape, 0)
        shift = jnp.where(
            r8 == 0, step * STEPS[a],
            jnp.where(r8 == 1, step * role_step[role], jnp.where(r8 == 2, step * STEPS[c], 0.0)),
        )
        rows_j[slot(a, role, c)] = block + shift

    def place_cols(blocks):
        stack = []
        for role, c in blocks:
            block = rows_j[slot(0, role, c)]
            r8 = lax.broadcasted_iota(jnp.int32, block.shape, 0)
            stack.append(jnp.where((r8 == 0) & (block > 0.5 * FAR_AWAY), -FAR_AWAY, block))
        if len(stack) < 16:
            stack.append(jnp.zeros((8 * (16 - len(stack)), atoms), f32))
        turned = jnp.transpose(jnp.concatenate(stack, 0))
        for n, where in enumerate(blocks):
            t = TARGETS.index(where)
            for axis in range(3):
                cols_i[t, axis] = jnp.broadcast_to(
                    turned[:, 8 * n + axis : 8 * n + axis + 1], (atoms, atoms)
                )

    own_t = TARGETS.index((OWN, 0))

    def forward_slots(slots, diag=False):
        for q in range(atoms // ROWS):
            at = slice(q * ROWS, (q + 1) * ROWS)
            xi, yi, zi = cols_i[own_t, 0, at], cols_i[own_t, 1, at], cols_i[own_t, 2, at]
            eye = jnp.where(row_id + q * ROWS == col_id, 4.0, 0.0) if diag else None
            for first, count, stride in slots:

                def one(n, unused, at=at, xi=xi, yi=yi, zi=zi, first=first, stride=stride, eye=eye):
                    s = first + n * stride
                    lanes = pl.ds(pl.multiple_of(s * atoms, atoms), atoms)

                    def store(k, value):
                        kern_f[k, at, lanes] = value

                    fill(rows_j[s], xi, yi, zi, store, eye)
                    return unused

                lax.fori_loop(0, count, one, 0)

    def backward_blocks(first, count, sources, diag=False):
        def one(n, unused):
            t = first + n // (atoms // ROWS)
            q = n % (atoms // ROWS)
            at = pl.ds(pl.multiple_of(q * ROWS, ROWS), ROWS)
            xi, yi, zi = cols_i[t, 0, at], cols_i[t, 1, at], cols_i[t, 2, at]
            eye = jnp.where(row_id + q * ROWS == col_id, 4.0, 0.0) if diag else None
            for a in sources:

                def store(k, value, a=a):
                    lo = (a * kinds + k) * atoms
                    kern_b[t, at, lo : lo + atoms] = value

                fill(rows_j[slot(a, OWN, 0)], xi, yi, zi, store, eye)
            return unused

        lax.fori_loop(0, count * (atoms // ROWS), one, 0)

    def pass_own(c):
        wait(("p", 0, OWN, c))
        for d in (1, 2):
            start(("p", flip[d], OWN, c))
        start(("p", 0, SIB, c))

    def pass_sib(c):
        for a in (1, 2):
            wait(("p", a, OWN, c))
            start(("p", a, SIB, c))

    def pass_far(c):
        wait(("p", 0, FAR, c))
        for d in (1, 2):
            start(("p", flip[d], FAR, c))

    def gather(first, count):
        lo, hi = first * atoms, (first + count) * atoms
        return jnp.dot(
            kern_f[:, :, lo:hi].reshape(kinds * atoms, hi - lo),
            proj[first : first + count].reshape(hi - lo, width),
            preferred_element_type=f32,
        ).reshape(kinds, atoms, width)

    def near_sum(c):
        for a in (0, 1, 2):
            wait(("p", a, SIB, c))
        msg[...] = gather(6 * c, 6) if c == 0 else msg[...] + gather(6 * c, 6)

    def far_sum(c):
        for a in (1, 2):
            wait(("p", a, FAR, c))
        msg[...] = msg[...] + gather(18 + 3 * c, 3)

    def take_far():
        wait(("p", 0, FAR, 0))
        for d in (1, 2):
            start(("p", 0, FAR, flip[d]))
        for d in (1, 2):
            start(("p", flip[d], FAR, 0))

    place_rows(0, OWN, 0)
    place_cols([(OWN, 0)])
    forward_slots([(slot(0, OWN, 0), 1, 1)], diag=True)
    backward_blocks(8, 1, (0,), diag=True)

    wait("c_sib")
    for d in (1, 2):
        sends(("c_gz1", flip[d]), coords.at[0, 0, 0:2], coords.at[0, flip[d], 0:2], to_gz[d])
    pass_sib(0)
    for c in (1, 2):
        pl.when(inside[c])(lambda c=c: pass_own(c))
    place_rows(0, SIB, 0)
    forward_slots([(slot(0, SIB, 0), 1, 1)])
    for d in (1, 2):
        copy_of(("c_gz2", flip[d]), coords.at[0, 0, FAR], coords.at[0, flip[d], FAR], to_gz[d])
        copy_of(
            ("c_gx1", flip[d]), coords.at[0, :, 0:2], coords.at[flip[d], :, 0:2], to_gx[d]
        )
        copy_of(("c_gx2", flip[d]), coords.at[0, :, FAR], coords.at[flip[d], :, FAR], to_gx[d])

    def coords_far():
        wait("c_far")
        for d in (1, 2):
            start(("c_gz2", flip[d]))
        for d in (1, 2):
            pl.when(cross[d])(lambda d=d: start(("p", 0, OWN, flip[d])))

    def coords_gz1():
        for c in (1, 2):
            wait(("c_gz1", c))
        for d in (1, 2):
            start(("c_gx1", flip[d]))
        for role in (OWN, SIB):
            for c in (1, 2):
                place_rows(0, role, c)
        forward_slots([(slot(0, OWN, c), 2, 1) for c in (1, 2)])

    def coords_gx1():
        for a in (1, 2):
            wait(("c_gx1", a))
            for role in (OWN, SIB):
                for c in (0, 1, 2):
                    place_rows(a, role, c)
        forward_slots([(slot(1, OWN, c), 4, 1) for c in (0, 1, 2)])

    def coords_gz2():
        for c in (1, 2):
            wait(("c_gz2", c))
        for d in (1, 2):
            start(("c_gx2", flip[d]))
        for c in (0, 1, 2):
            place_rows(0, FAR, c)
        forward_slots([(slot(0, FAR, 0), 1, 1)])

    def coords_gx2():
        for a in (1, 2):
            wait(("c_gx2", a))
            for c in (0, 1, 2):
                place_rows(a, FAR, c)
        forward_slots([(slot(1, FAR, 0), 8, 1)])

    def backward_near():
        place_cols([where for where in TARGETS if where != (OWN, 0)])
        backward_blocks(2, 5, (0, 1, 2))
        backward_blocks(8, 1, (1, 2))

    def backward_far():
        backward_blocks(0, 2, (0, 1, 2))
        backward_blocks(7, 1, (0, 1, 2))

    def plain():
        coords_gz1()
        for c in (1, 2):
            pl.when(inside[c])(lambda c=c: pass_sib(c))
        coords_far()
        coords_gx1()
        near_sum(0)
        for c in (1, 2):
            pl.when(inside[c])(lambda c=c: near_sum(c))
        for c in (1, 2):
            pl.when(cross[c])(lambda c=c: pass_own(c))
        take_far()
        coords_gz2()
        backward_near()
        for c in (1, 2):
            pl.when(inside[c])(lambda c=c: pass_far(c))
        for c in (1, 2):
            pl.when(cross[c])(lambda c=c: pass_sib(c))
        for c in (1, 2):
            pl.when(cross[c])(lambda c=c: pass_far(c))
        coords_gx2()
        backward_far()
        for c in (1, 2):
            pl.when(cross[c])(lambda c=c: near_sum(c))
        far_sum(0)
        for c in (1, 2):
            pl.when(inside[c])(lambda c=c: far_sum(c))
        for c in (1, 2):
            pl.when(cross[c])(lambda c=c: far_sum(c))

    def at_seam(c):
        other = flip[c]
        coords_far()
        pass_sib(other)
        coords_gz1()
        take_far()
        coords_gx1()
        near_sum(0)
        coords_gz2()
        pass_own(c)
        near_sum(other)
        pass_far(other)
        coords_gx2()
        pass_sib(c)
        far_sum(0)
        pass_far(c)
        near_sum(c)
        far_sum(other)
        far_sum(c)

    pl.when((gz != 0) & (gz != nz - 1))(plain)
    for c in (1, 2):
        pl.when(seam[c])(lambda c=c: at_seam(c))

    weights = [
        radial_ref[b : b + 1] * math.exp(-GAMMA * (b / (bases - 1)) ** 2) for b in range(bases)
    ]
    readout = readout_ref[...]
    info = jnp.concatenate(
        [
            targ_ref[0], targ_ref[1], targ_ref[2],
            jnp.where(occ_row, mask_ref[...].astype(f32) * LOSS_WEIGHT, 0.0),
            jnp.zeros((atoms - 4, atoms), f32),
        ],
        0,
    )
    zcols[...] = jnp.transpose(info)
    for q in range(atoms // ROWS):
        at = slice(q * ROWS, (q + 1) * ROWS)
        pre = weights[0] * msg[0, at]
        for b in range(1, bases):
            pre = pre + weights[b] * msg[b, at]
        gate = jax.nn.sigmoid(pre)
        gates = readout * gate
        cols = zcols[at]
        scale = cols[:, 3:4]
        pull = jnp.zeros_like(pre)
        out = jnp.zeros((ROWS, atoms), f32)
        for c in range(3):
            vec = msg[bases + c, at]
            pred = jnp.sum(gates * vec, axis=1, keepdims=True)
            err = scale * (pred - cols[:, c : c + 1])
            pull = pull + err * vec
            out = jnp.where(col_id == c, pred, out)
            out = jnp.where(col_id == 3 + c, err, out)
        zcols[at] = out
        acts[0, 0, at] = (pull * readout * gate * (1.0 - gate)).astype(bf16)
        acts[0, 1, at] = gates.astype(bf16)
    turned = jnp.transpose(zcols[...])
    for c in range(3):
        pred_ref[c] = turned[c : c + 1]
    errs[0] = turned[0:8]

    for d in (1, 2):
        sends(("act", flip[d]), acts.at[0], acts.at[flip[d]], to_gx[d])
        sends(("err", flip[d]), errs.at[0], errs.at[flip[d]], to_gx[d])

    def build_rhs(a, cols, first):
        for q in range(atoms // ROWS):
            at = slice(q * ROWS, (q + 1) * ROWS)
            slope = acts[a, 0, at].astype(f32)
            gates = acts[a, 1, at].astype(f32)
            for b in range(bases):
                rhs[a * kinds + b, at] = (weights[b] * slope).astype(bf16)
            for c in range(3):
                err = cols[q * ROWS : (q + 1) * ROWS, first + c : first + c + 1]
                rhs[a * kinds + bases + c, at] = (gates * (-err)).astype(bf16)

    def late_backward():
        backward_near()
        backward_far()

    build_rhs(0, zcols[...], 3)
    part = kinds * atoms
    pl.when((gz == 0) | (gz == nz - 1))(late_backward)
    partial[...] = jnp.dot(
        kern_b[:, :, :part].reshape(9 * atoms, part),
        rhs[0:kinds].reshape(part, width),
        preferred_element_type=f32,
    ).reshape(9, atoms, width)
    for a in (1, 2):
        wait(("act", a))
        wait(("err", a))
    zcols[...] = jnp.transpose(
        jnp.concatenate([errs[1], errs[2], jnp.zeros((atoms - 16, atoms), f32)], 0)
    )
    build_rhs(1, zcols[...], 3)
    build_rhs(2, zcols[...], 11)

    def totals(first, count):
        return partial[first : first + count] + jnp.dot(
            kern_b[first : first + count, :, part:].reshape(count * atoms, 2 * part),
            rhs[kinds:].reshape(2 * part, width),
            preferred_element_type=f32,
        ).reshape(count, atoms, width)

    part_gz[1] = totals(0, 2).astype(bf16)
    for d in (1, 2):
        gx_d, gy_d, gz_d = to_gz[d]
        device = (gx_d, gy_d + on_seam[d] * (far_gy - gy_d), gz_d)
        sends(("far_gz", flip[d]), part_gz.at[1, d - 1], got_gz.at[1, flip[d] - 1], device)
    part_sib[...] = totals(2, 3).astype(bf16)
    sends("sib", part_sib, got_sib, sib)
    partial[5:7] = totals(5, 2)
    partial[7] = totals(7, 1)[0]
    wait("sib")
    part_gz[0] = (partial[5:7] + got_sib[0:2].astype(f32)).astype(bf16)
    for d in (1, 2):
        sends(("own_gz", flip[d]), part_gz.at[0, d - 1], got_gz.at[0, flip[d] - 1], to_gz[d])

    def add_far_gz(c, n):
        wait(("far_gz", c))
        partial[n] = partial[n] + got_gz[1, c - 1].astype(f32)

    for c in (1, 2):
        pl.when(no_seam[c])(lambda c=c: add_far_gz(c, 7))
    part_far[...] = partial[7].astype(bf16)
    sends("far", part_far, got_far, far)
    partial[8] = totals(8, 1)[0] + got_sib[2].astype(f32)
    for c in (1, 2):
        wait(("own_gz", c))
    partial[8] = partial[8] + got_gz[0, 0].astype(f32) + got_gz[0, 1].astype(f32)
    for c in (1, 2):
        pl.when(seam[c])(lambda c=c: add_far_gz(c, 8))
    wait("far")
    back_ref[...] = (partial[8] + got_far[...].astype(f32)).astype(bf16)
    for copy in copies.values():
        copy.wait_send()


COPIES = 26 + 10 + 4 + 6


def on_device(offsets, features, counts, mask, targets, w_in, radial, readout):
    atoms, width = features.shape[3:]
    bases = radial.shape[0]
    kinds = bases + 3
    f32, bf16 = jnp.float32, jnp.bfloat16
    vmem = pl.BlockSpec(memory_space=pltpu.VMEM)
    back, pred = pl.pallas_call(
        kernel,
        out_shape=(
            jax.ShapeDtypeStruct((atoms, width), bf16),
            jax.ShapeDtypeStruct((3, 1, atoms), f32),
        ),
        in_specs=[pl.BlockSpec(memory_space=pltpu.SMEM)] + [pl.BlockSpec(memory_space=pl.ANY)] * 7,
        out_specs=(vmem, vmem),
        scratch_shapes=[
            pltpu.VMEM((3, 1, atoms), f32),
            pltpu.VMEM((atoms, width), bf16),
            pltpu.VMEM((1, atoms), jnp.int32),
            pltpu.VMEM((3, 1, atoms), f32),
            pltpu.VMEM(w_in.shape, bf16),
            pltpu.VMEM(radial.shape, f32),
            pltpu.VMEM((1, width), f32),
            pltpu.VMEM((27, atoms, width), bf16),
            pltpu.VMEM((3, 3, 3, 8, atoms), f32),
            pltpu.VMEM((27, 8, atoms), f32),
            pltpu.VMEM((9, 3, atoms, atoms), f32),
            pltpu.VMEM((kinds, atoms, 27 * atoms), bf16),
            pltpu.VMEM((9, atoms, 3 * kinds * atoms), bf16),
            pltpu.VMEM((kinds, atoms, width), f32),
            pltpu.VMEM((3 * kinds, atoms, width), bf16),
            pltpu.VMEM((9, atoms, width), f32),
            pltpu.VMEM((3, 2, atoms, width), bf16),
            pltpu.VMEM((3, 8, atoms), f32),
            pltpu.VMEM((atoms, atoms), f32),
            pltpu.VMEM((3, atoms, width), bf16),
            pltpu.VMEM((3, atoms, width), bf16),
            pltpu.VMEM((2, 2, atoms, width), bf16),
            pltpu.VMEM((2, 2, atoms, width), bf16),
            pltpu.VMEM((atoms, width), bf16),
            pltpu.VMEM((atoms, width), bf16),
            pltpu.SemaphoreType.DMA((COPIES,)),
            pltpu.SemaphoreType.DMA((COPIES,)),
            pltpu.SemaphoreType.DMA((7,)),
        ],
        compiler_params=pltpu.CompilerParams(
            collective_id=0, has_side_effects=True, vmem_limit_bytes=60 << 20
        ),
        name="message_passing",
    )(
        counts.reshape(1),
        offsets.reshape(3, 1, atoms),
        features.reshape(atoms, width),
        mask.reshape(1, atoms),
        targets.reshape(3, 1, atoms),
        w_in,
        radial,
        readout.reshape(1, width),
    )
    grad = lax.dot_general(
        back, w_in, (((1,), (1,)), ((), ())), preferred_element_type=jnp.float32
    )
    return (pred.reshape(1, 1, 1, 3, atoms), grad.reshape(1, 1, 1, atoms, width))


def solution(mesh):
    in_specs = (
        P("gx", "gy", "gz", None, None),
        P("gx", "gy", "gz", None, None),
        P("gx", "gy", "gz"),
        P("gx", "gy", "gz", None),
        P("gx", "gy", "gz", None, None),
        P(),
        P(),
        P(),
    )
    out_specs = (P("gx", "gy", "gz", None, None), P("gx", "gy", "gz", None, None))
    return jax.shard_map(
        on_device, mesh=mesh, in_specs=in_specs, out_specs=out_specs, check_vma=False
    )
```

```python
import math

import jax
import jax.numpy as jnp
from jax import lax
from jax.experimental import pallas as pl
from jax.experimental.pallas import tpu as pltpu
from jax.sharding import PartitionSpec as P

EDGE = 10.0
CUT = 5.0
GAMMA = 20.0
LOSS_WEIGHT = 16.0
FAR_AWAY = 1.0e4
MESH = pl.DeviceIdType.MESH
ROWS = 32
RUN_X = 4

OWN, SIB, FAR = 0, 1, 2
STEPS = (0, -1, 1)
TARGETS = ((FAR, 1), (FAR, 2), (SIB, 1), (SIB, 2), (SIB, 0), (OWN, 1), (OWN, 2), (FAR, 0), (OWN, 0))


def slot(a, role, c):
    return 18 + c * 3 + a if role == FAR else c * 6 + a * 2 + role


def kernel(
    count_ref, offs_in, feat_in, mask_in, targ_in, w_in, radial_in, readout_in,
    back_ref, pred_ref,
    offs_ref, feat_ref, mask_ref, targ_ref, w_ref, radial_ref, readout_ref,
    proj, coords, rows_j, cols_i, kern_f, kern_b, msg, rhs, partial, acts, errs, zcols,
    part_sib, got_sib, part_gz, got_gz, part_far, got_far, part_seam, got_seam,
    send_sem, recv_sem, load_sem,
):
    atoms, width = feat_ref.shape
    bases = radial_ref.shape[0]
    kinds = bases + 3
    f32, bf16 = jnp.float32, jnp.bfloat16
    gx, gy, gz = lax.axis_index("gx"), lax.axis_index("gy"), lax.axis_index("gz")
    nx, ny, nz = lax.axis_size("gx"), lax.axis_size("gy"), lax.axis_size("gz")
    core = gy % 2
    sib_gy = gy + 1 - 2 * core
    far_gy = (gy + ny - 1 + 2 * core) % ny
    sib = (gx, sib_gy, gz)
    far = (gx, far_gy, gz)
    to_gx = {1: ((gx + nx - 1) % nx, gy, gz), 2: ((gx + 1) % nx, gy, gz)}
    to_gz = {1: (gx, gy, (gz + nz - 1) % nz), 2: (gx, gy, (gz + 1) % nz)}
    flip = {1: 2, 2: 1}
    cross = {1: gz % RUN_X == 0, 2: gz % RUN_X == RUN_X - 1}
    inside = {1: gz % RUN_X != 0, 2: gz % RUN_X != RUN_X - 1}
    seam = {1: gz == 0, 2: gz == nz - 1}
    no_seam = {1: gz != 0, 2: gz != nz - 1}
    edge = {1: (gz % RUN_X == 0) & (gz != 0), 2: (gz % RUN_X == RUN_X - 1) & (gz != nz - 1)}
    sib_step = (1 - 2 * core).astype(f32)
    role_step = (0.0, sib_step, -sib_step)

    barrier = pltpu.get_barrier_semaphore()
    for other in (far, to_gz[1], to_gz[2], to_gx[1], to_gx[2], sib):
        pl.semaphore_signal(barrier, inc=1, device_id=other, device_id_type=MESH)

    loads = [
        pltpu.make_async_copy(src, dst, load_sem.at[n])
        for n, (src, dst) in enumerate(
            (
                (feat_in, feat_ref), (w_in, w_ref), (offs_in, offs_ref), (mask_in, mask_ref),
                (targ_in, targ_ref), (radial_in, radial_ref), (readout_in, readout_ref),
            )
        )
    ]
    for load in loads:
        load.start()

    copies = {}

    def copy_of(name, src, dst, device):
        index = len(copies)
        copies[name] = pltpu.make_async_remote_copy(
            src_ref=src, dst_ref=dst, send_sem=send_sem.at[index], recv_sem=recv_sem.at[index],
            device_id=device, device_id_type=MESH,
        )

    def wait(name):
        copies[name].wait_recv()

    def start(name):
        copies[name].start()

    def sends(name, src, dst, device):
        copy_of(name, src, dst, device)
        start(name)

    here = lambda a, role, c: proj.at[slot(a, role, c)]
    half = atoms // 2
    part_of = lambda a, role, c, h: proj.at[slot(a, role, c), h * half : (h + 1) * half]
    for h in (0, 1):
        copy_of(("f", 0, 0, h), part_of(0, OWN, 0, h), part_of(0, FAR, 0, h), far)
    for d in (1, 2):
        e = flip[d]
        copy_of(("p", 0, OWN, e), here(0, OWN, 0), here(0, OWN, e), to_gz[d])
        for h in (0, 1):
            copy_of(("f", 0, e, h), part_of(0, FAR, 0, h), part_of(0, FAR, e, h), to_gz[d])
        for c in (0, 1, 2):
            copy_of(("p", e, OWN, c), here(0, OWN, c), here(e, OWN, c), to_gx[d])
            for h in (0, 1):
                copy_of(("f", e, c, h), part_of(0, FAR, c, h), part_of(e, FAR, c, h), to_gx[d])
    for a in (0, 1, 2):
        for c in (0, 1, 2):
            copy_of(("p", a, SIB, c), here(a, OWN, c), here(a, SIB, c), sib)

    for load in loads:
        load.wait()
    lane = lax.broadcasted_iota(jnp.int32, (1, atoms), 1)
    occ_row = lane < count_ref[0]
    own = [offs_ref[axis] * (1.0 / CUT) for axis in range(3)]
    coords[0, 0, OWN] = jnp.concatenate(
        [jnp.where(occ_row, own[0], FAR_AWAY), own[1], own[2], jnp.zeros((5, atoms), f32)], 0
    )
    proj[slot(0, OWN, 0)] = jnp.dot(
        feat_ref[...], w_ref[...], preferred_element_type=f32
    ).astype(bf16)

    pl.semaphore_wait(barrier, 6)

    sends("c_far", coords.at[0, 0, OWN], coords.at[0, 0, FAR], far)
    for h in (0, 1):
        start(("f", 0, 0, h))
    sends("c_sib", coords.at[0, 0, OWN], coords.at[0, 0, SIB], sib)
    for d in (1, 2):
        pl.when(inside[d])(lambda d=d: start(("p", 0, OWN, flip[d])))
    for d in (1, 2):
        start(("p", flip[d], OWN, 0))
    start(("p", 0, SIB, 0))

    row_id = lax.broadcasted_iota(jnp.int32, (ROWS, atoms), 0)
    col_id = lax.broadcasted_iota(jnp.int32, (ROWS, atoms), 1)
    step = 2.0 * EDGE / (2.0 * CUT)

    def fill(block, xi, yi, zi, store, diag=None):
        dx = block[0:1] - xi
        dy = block[1:2] - yi
        dz = block[2:3] - zi
        ratio = dx * dx + dy * dy + dz * dz
        if diag is not None:
            ratio = ratio + diag
        room = jnp.maximum(1.0 - ratio, 0.0)
        near = 1.0 - room
        env = room * room
        grow = jnp.exp((2.0 * GAMMA / (bases - 1)) * near)
        value = env * jnp.exp(-GAMMA * (near * near))
        for k in range(bases):
            store(k, value.astype(bf16))
            if k < bases - 1:
                value = value * grow
        store(bases, (env * dx).astype(bf16))
        store(bases + 1, (env * dy).astype(bf16))
        store(bases + 2, (env * dz).astype(bf16))

    def place_rows(a, role, c):
        block = coords[a, c, role]
        r8 = lax.broadcasted_iota(jnp.int32, block.shape, 0)
        shift = jnp.where(
            r8 == 0, step * STEPS[a],
            jnp.where(r8 == 1, step * role_step[role], jnp.where(r8 == 2, step * STEPS[c], 0.0)),
        )
        rows_j[slot(a, role, c)] = block + shift

    def place_cols(blocks):
        stack = []
        for role, c in blocks:
            block = rows_j[slot(0, role, c)]
            r8 = lax.broadcasted_iota(jnp.int32, block.shape, 0)
            stack.append(jnp.where((r8 == 0) & (block > 0.5 * FAR_AWAY), -FAR_AWAY, block))
        if len(stack) < 16:
            stack.append(jnp.zeros((8 * (16 - len(stack)), atoms), f32))
        turned = jnp.transpose(jnp.concatenate(stack, 0))
        for n, where in enumerate(blocks):
            t = TARGETS.index(where)
            for axis in range(3):
                cols_i[t, axis] = jnp.broadcast_to(
                    turned[:, 8 * n + axis : 8 * n + axis + 1], (atoms, atoms)
                )

    own_t = TARGETS.index((OWN, 0))

    def forward_slots(slots, diag=False):
        for q in range(atoms // ROWS):
            at = slice(q * ROWS, (q + 1) * ROWS)
            xi, yi, zi = cols_i[own_t, 0, at], cols_i[own_t, 1, at], cols_i[own_t, 2, at]
            eye = jnp.where(row_id + q * ROWS == col_id, 4.0, 0.0) if diag else None
            for first, count, stride in slots:

                def one(n, unused, at=at, xi=xi, yi=yi, zi=zi, first=first, stride=stride, eye=eye):
                    s = first + n * stride
                    lanes = pl.ds(pl.multiple_of(s * atoms, atoms), atoms)

                    def store(k, value):
                        kern_f[k, at, lanes] = value

                    fill(rows_j[s], xi, yi, zi, store, eye)
                    return unused

                lax.fori_loop(0, count, one, 0)

    def backward_blocks(first, count, sources, diag=False):
        def one(n, unused):
            t = first + n // (atoms // ROWS)
            q = n % (atoms // ROWS)
            at = pl.ds(pl.multiple_of(q * ROWS, ROWS), ROWS)
            xi, yi, zi = cols_i[t, 0, at], cols_i[t, 1, at], cols_i[t, 2, at]
            eye = jnp.where(row_id + q * ROWS == col_id, 4.0, 0.0) if diag else None
            for a in sources:

                def store(k, value, a=a):
                    lo = (a * kinds + k) * atoms
                    kern_b[t, at, lo : lo + atoms] = value

                fill(rows_j[slot(a, OWN, 0)], xi, yi, zi, store, eye)
            return unused

        lax.fori_loop(0, count * (atoms // ROWS), one, 0)

    def pass_own(c):
        wait(("p", 0, OWN, c))
        for d in (1, 2):
            start(("p", flip[d], OWN, c))
        start(("p", 0, SIB, c))

    def pass_sib(c):
        for a in (1, 2):
            wait(("p", a, OWN, c))
            start(("p", a, SIB, c))

    def pass_far(c):
        for h in (0, 1):
            wait(("f", 0, c, h))
            for d in (1, 2):
                start(("f", flip[d], c, h))

    def gather(first, count):
        lo, hi = first * atoms, (first + count) * atoms
        return jnp.dot(
            kern_f[:, :, lo:hi].reshape(kinds * atoms, hi - lo),
            proj[first : first + count].reshape(hi - lo, width),
            preferred_element_type=f32,
        ).reshape(kinds, atoms, width)

    def near_sum(c):
        for a in (0, 1, 2):
            wait(("p", a, SIB, c))
        msg[...] = gather(6 * c, 6) if c == 0 else msg[...] + gather(6 * c, 6)

    def far_sum(c):
        for a in (1, 2):
            for h in (0, 1):
                wait(("f", a, c, h))
        msg[...] = msg[...] + gather(18 + 3 * c, 3)

    def take_far():
        for h in (0, 1):
            wait(("f", 0, 0, h))
            for d in (1, 2):
                start(("f", 0, flip[d], h))
            for d in (1, 2):
                start(("f", flip[d], 0, h))

    place_rows(0, OWN, 0)
    place_cols([(OWN, 0)])
    forward_slots([(slot(0, OWN, 0), 1, 1)], diag=True)
    backward_blocks(8, 1, (0,), diag=True)

    wait("c_sib")
    for d in (1, 2):
        sends(("c_gz1", flip[d]), coords.at[0, 0, 0:2], coords.at[0, flip[d], 0:2], to_gz[d])
    pass_sib(0)
    for c in (1, 2):
        pl.when(inside[c])(lambda c=c: pass_own(c))
    place_rows(0, SIB, 0)
    forward_slots([(slot(0, SIB, 0), 1, 1)])
    for d in (1, 2):
        copy_of(("c_gz2", flip[d]), coords.at[0, 0, FAR], coords.at[0, flip[d], FAR], to_gz[d])
        copy_of(
            ("c_gx1", flip[d]), coords.at[0, :, 0:2], coords.at[flip[d], :, 0:2], to_gx[d]
        )
        copy_of(("c_gx2", flip[d]), coords.at[0, :, FAR], coords.at[flip[d], :, FAR], to_gx[d])

    def coords_far():
        wait("c_far")
        for d in (1, 2):
            start(("c_gz2", flip[d]))
        for d in (1, 2):
            pl.when(cross[d])(lambda d=d: start(("p", 0, OWN, flip[d])))

    def coords_gz1():
        for c in (1, 2):
            wait(("c_gz1", c))
        for d in (1, 2):
            start(("c_gx1", flip[d]))
        for role in (OWN, SIB):
            for c in (1, 2):
                place_rows(0, role, c)
        forward_slots([(slot(0, OWN, c), 2, 1) for c in (1, 2)])

    def coords_gx1():
        for a in (1, 2):
            wait(("c_gx1", a))
            for role in (OWN, SIB):
                for c in (0, 1, 2):
                    place_rows(a, role, c)
        forward_slots([(slot(1, OWN, c), 4, 1) for c in (0, 1, 2)])

    def coords_gz2():
        for c in (1, 2):
            wait(("c_gz2", c))
        for d in (1, 2):
            start(("c_gx2", flip[d]))
        for c in (0, 1, 2):
            place_rows(0, FAR, c)
        forward_slots([(slot(0, FAR, 0), 1, 1)])

    def coords_gx2():
        for a in (1, 2):
            wait(("c_gx2", a))
            for c in (0, 1, 2):
                place_rows(a, FAR, c)
        forward_slots([(slot(1, FAR, 0), 8, 1)])

    def backward_near():
        place_cols([where for where in TARGETS if where != (OWN, 0)])
        backward_blocks(2, 5, (0, 1, 2))
        backward_blocks(8, 1, (1, 2))

    def backward_far():
        backward_blocks(0, 2, (0, 1, 2))
        backward_blocks(7, 1, (0, 1, 2))

    def plain():
        coords_gz1()
        for c in (1, 2):
            pl.when(inside[c])(lambda c=c: pass_sib(c))
        coords_far()
        coords_gx1()
        near_sum(0)
        for c in (1, 2):
            pl.when(inside[c])(lambda c=c: near_sum(c))
        for c in (1, 2):
            pl.when(cross[c])(lambda c=c: pass_own(c))
        take_far()
        coords_gz2()
        backward_near()
        for c in (1, 2):
            pl.when(inside[c])(lambda c=c: pass_far(c))
        for c in (1, 2):
            pl.when(cross[c])(lambda c=c: pass_sib(c))
        for c in (1, 2):
            pl.when(cross[c])(lambda c=c: pass_far(c))
        coords_gx2()
        backward_far()
        for c in (1, 2):
            pl.when(cross[c])(lambda c=c: near_sum(c))
        far_sum(0)
        for c in (1, 2):
            pl.when(inside[c])(lambda c=c: far_sum(c))
        for c in (1, 2):
            pl.when(cross[c])(lambda c=c: far_sum(c))

    def at_seam(c):
        other = flip[c]
        coords_far()
        pass_sib(other)
        coords_gz1()
        take_far()
        coords_gx1()
        near_sum(0)
        coords_gz2()
        pass_own(c)
        near_sum(other)
        pass_far(other)
        coords_gx2()
        pass_sib(c)
        pass_far(c)
        far_sum(0)
        near_sum(c)
        far_sum(other)
        far_sum(c)

    pl.when((gz != 0) & (gz != nz - 1))(plain)
    for c in (1, 2):
        pl.when(seam[c])(lambda c=c: at_seam(c))

    weights = [
        radial_ref[b : b + 1] * math.exp(-GAMMA * (b / (bases - 1)) ** 2) for b in range(bases)
    ]
    readout = readout_ref[...]
    info = jnp.concatenate(
        [
            targ_ref[0], targ_ref[1], targ_ref[2],
            jnp.where(occ_row, mask_ref[...].astype(f32) * LOSS_WEIGHT, 0.0),
            jnp.zeros((atoms - 4, atoms), f32),
        ],
        0,
    )
    zcols[...] = jnp.transpose(info)
    for q in range(atoms // ROWS):
        at = slice(q * ROWS, (q + 1) * ROWS)
        pre = weights[0] * msg[0, at]
        for b in range(1, bases):
            pre = pre + weights[b] * msg[b, at]
        gate = jax.nn.sigmoid(pre)
        gates = readout * gate
        cols = zcols[at]
        scale = cols[:, 3:4]
        pull = jnp.zeros_like(pre)
        out = jnp.zeros((ROWS, atoms), f32)
        for c in range(3):
            vec = msg[bases + c, at]
            pred = jnp.sum(gates * vec, axis=1, keepdims=True)
            err = scale * (pred - cols[:, c : c + 1])
            pull = pull + err * vec
            out = jnp.where(col_id == c, pred, out)
            out = jnp.where(col_id == 3 + c, err, out)
        zcols[at] = out
        acts[0, 0, at] = (pull * readout * gate * (1.0 - gate)).astype(bf16)
        acts[0, 1, at] = gates.astype(bf16)
    turned = jnp.transpose(zcols[...])
    for c in range(3):
        pred_ref[c] = turned[c : c + 1]
    errs[0] = turned[0:8]

    for d in (1, 2):
        sends(("act", flip[d]), acts.at[0], acts.at[flip[d]], to_gx[d])
        sends(("err", flip[d]), errs.at[0], errs.at[flip[d]], to_gx[d])

    def build_rhs(a, cols, first):
        for q in range(atoms // ROWS):
            at = slice(q * ROWS, (q + 1) * ROWS)
            slope = acts[a, 0, at].astype(f32)
            gates = acts[a, 1, at].astype(f32)
            for b in range(bases):
                rhs[a * kinds + b, at] = (weights[b] * slope).astype(bf16)
            for c in range(3):
                err = cols[q * ROWS : (q + 1) * ROWS, first + c : first + c + 1]
                rhs[a * kinds + bases + c, at] = (gates * (-err)).astype(bf16)

    def late_backward():
        backward_near()
        backward_far()

    build_rhs(0, zcols[...], 3)
    part = kinds * atoms
    copy_of("seam", part_seam, got_seam, (gx, far_gy, nz - 1 - gz))
    pl.when((gz == 0) | (gz == nz - 1))(late_backward)
    partial[...] = jnp.dot(
        kern_b[:, :, :part].reshape(9 * atoms, part),
        rhs[0:kinds].reshape(part, width),
        preferred_element_type=f32,
    ).reshape(9, atoms, width)
    for a in (1, 2):
        wait(("act", a))
        wait(("err", a))
    zcols[...] = jnp.transpose(
        jnp.concatenate([errs[1], errs[2], jnp.zeros((atoms - 16, atoms), f32)], 0)
    )
    build_rhs(1, zcols[...], 3)
    build_rhs(2, zcols[...], 11)

    def totals(first, count):
        return partial[first : first + count] + jnp.dot(
            kern_b[first : first + count, :, part:].reshape(count * atoms, 2 * part),
            rhs[kinds:].reshape(2 * part, width),
            preferred_element_type=f32,
        ).reshape(count, atoms, width)

    for d in (1, 2):
        copy_of(("far_gz", flip[d]), part_gz.at[1, d - 1], got_gz.at[1, flip[d] - 1], to_gz[d])
        copy_of(("own_gz", flip[d]), part_gz.at[0, d - 1], got_gz.at[0, flip[d] - 1], to_gz[d])
    copy_of("far", part_far, got_far, far)

    def send_far(steps):
        total = partial[7]
        for c in steps:
            wait(("far_gz", c))
            total = total + got_gz[1, c - 1].astype(f32)
        part_far[...] = total.astype(bf16)
        start("far")

    def seam_first(c):
        other = flip[c]
        part_gz[1, other - 1] = totals(other - 1, 1)[0].astype(bf16)
        start(("far_gz", c))
        part_seam[...] = totals(c - 1, 1)[0].astype(bf16)
        start("seam")
        partial[7] = totals(7, 1)[0]
        send_far((other,))

    def plain_first():
        part_gz[1] = totals(0, 2).astype(bf16)
        for c in (1, 2):
            start(("far_gz", c))

    def plain_far():
        partial[7] = totals(7, 1)[0]
        send_far((1, 2))

    no_seams = (gz != 0) & (gz != nz - 1)
    for c in (1, 2):
        pl.when(seam[c])(lambda c=c: seam_first(c))
    pl.when(no_seams)(plain_first)
    part_sib[...] = totals(2, 3).astype(bf16)
    sends("sib", part_sib, got_sib, sib)
    pl.when(no_seams)(plain_far)
    partial[5:7] = totals(5, 2)
    wait("sib")
    part_gz[0] = (partial[5:7] + got_sib[0:2].astype(f32)).astype(bf16)
    for d in (1, 2):
        start(("own_gz", flip[d]))
    partial[8] = totals(8, 1)[0] + got_sib[2].astype(f32)

    for c in (1, 2):
        wait(("own_gz", c))
    partial[8] = partial[8] + got_gz[0, 0].astype(f32) + got_gz[0, 1].astype(f32)

    def add_seam():
        wait("seam")
        partial[8] = partial[8] + got_seam[...].astype(f32)

    pl.when((gz == 0) | (gz == nz - 1))(add_seam)
    wait("far")
    back_ref[...] = (partial[8] + got_far[...].astype(f32)).astype(bf16)
    for name, copy in copies.items():
        if name == "seam":
            pl.when((gz == 0) | (gz == nz - 1))(copy.wait_send)
        elif name[0] == "far_gz":
            pl.when(no_seam[flip[name[1]]])(copy.wait_send)
        else:
            copy.wait_send()


COPIES = 26 + 9 + 10 + 4 + 6 + 1


def on_device(offsets, features, counts, mask, targets, w_in, radial, readout):
    atoms, width = features.shape[3:]
    bases = radial.shape[0]
    kinds = bases + 3
    f32, bf16 = jnp.float32, jnp.bfloat16
    vmem = pl.BlockSpec(memory_space=pltpu.VMEM)
    back, pred = pl.pallas_call(
        kernel,
        out_shape=(
            jax.ShapeDtypeStruct((atoms, width), bf16),
            jax.ShapeDtypeStruct((3, 1, atoms), f32),
        ),
        in_specs=[pl.BlockSpec(memory_space=pltpu.SMEM)] + [pl.BlockSpec(memory_space=pl.ANY)] * 7,
        out_specs=(vmem, vmem),
        scratch_shapes=[
            pltpu.VMEM((3, 1, atoms), f32),
            pltpu.VMEM((atoms, width), bf16),
            pltpu.VMEM((1, atoms), jnp.int32),
            pltpu.VMEM((3, 1, atoms), f32),
            pltpu.VMEM(w_in.shape, bf16),
            pltpu.VMEM(radial.shape, f32),
            pltpu.VMEM((1, width), f32),
            pltpu.VMEM((27, atoms, width), bf16),
            pltpu.VMEM((3, 3, 3, 8, atoms), f32),
            pltpu.VMEM((27, 8, atoms), f32),
            pltpu.VMEM((9, 3, atoms, atoms), f32),
            pltpu.VMEM((kinds, atoms, 27 * atoms), bf16),
            pltpu.VMEM((9, atoms, 3 * kinds * atoms), bf16),
            pltpu.VMEM((kinds, atoms, width), f32),
            pltpu.VMEM((3 * kinds, atoms, width), bf16),
            pltpu.VMEM((9, atoms, width), f32),
            pltpu.VMEM((3, 2, atoms, width), bf16),
            pltpu.VMEM((3, 8, atoms), f32),
            pltpu.VMEM((atoms, atoms), f32),
            pltpu.VMEM((3, atoms, width), bf16),
            pltpu.VMEM((3, atoms, width), bf16),
            pltpu.VMEM((2, 2, atoms, width), bf16),
            pltpu.VMEM((2, 2, atoms, width), bf16),
            pltpu.VMEM((atoms, width), bf16),
            pltpu.VMEM((atoms, width), bf16),
            pltpu.VMEM((atoms, width), bf16),
            pltpu.VMEM((atoms, width), bf16),
            pltpu.SemaphoreType.DMA((COPIES,)),
            pltpu.SemaphoreType.DMA((COPIES,)),
            pltpu.SemaphoreType.DMA((7,)),
        ],
        compiler_params=pltpu.CompilerParams(
            collective_id=0, has_side_effects=True, vmem_limit_bytes=60 << 20
        ),
        name="message_passing",
    )(
        counts.reshape(1),
        offsets.reshape(3, 1, atoms),
        features.reshape(atoms, width),
        mask.reshape(1, atoms),
        targets.reshape(3, 1, atoms),
        w_in,
        radial,
        readout.reshape(1, width),
    )
    grad = lax.dot_general(
        back, w_in, (((1,), (1,)), ((), ())), preferred_element_type=jnp.float32
    )
    return (pred.reshape(1, 1, 1, 3, atoms), grad.reshape(1, 1, 1, atoms, width))


def solution(mesh):
    in_specs = (
        P("gx", "gy", "gz", None, None),
        P("gx", "gy", "gz", None, None),
        P("gx", "gy", "gz"),
        P("gx", "gy", "gz", None),
        P("gx", "gy", "gz", None, None),
        P(),
        P(),
        P(),
    )
    out_specs = (P("gx", "gy", "gz", None, None), P("gx", "gy", "gz", None, None))
    return jax.shard_map(
        on_device, mesh=mesh, in_specs=in_specs, out_specs=out_specs, check_vma=False
    )
```
